512 devices in a mesh: seq: 32 (over y, z_hi), heads: 16 (over z_lo, x, core).
Axes of the slice: x: 4, y: 8, z: 8 (z_hi: 4, z_lo: 2; z = z_hi * 2 + z_lo), core: 2. Of those that a mesh axis runs over, the one named last changes fastest.
Arguments:
- fwd_tokens: bfloat16 [8192, 4096], P('seq'), may hold values from -6 to 6
- bwd_tokens: bfloat16 [8192, 4096], P('seq'), may hold values from -6 to 6
- qkv_weight: bfloat16 [4096, 12288], P('seq', 'heads'), may hold values from -0.09375 to 0.09375
- head_gain: float32 [4096], P('heads'), may hold values from 0.1 to 1.9
- out_cotangent: float32 [8192, 4096], P('seq', 'heads'), may hold values from -6 to 6
- initial_state: float32 [2, 16, 256, 256], P(None, 'heads'), may hold values from -192 to 192
Outputs:
- fwd_output: float32 [8192, 4096], P('seq', 'heads')
- bwd_token_grad: bfloat16 [8192, 4096], P('seq', 'heads')
The draws below stay inside these ranges and needn't reach their ends.
All inputs are finite; a program needn't handle non-finite values.
Results may differ from the reference program's by a relative error of at most 0.02.
Values may be sent and summed in bfloat16 or wider, within the bound.
No kernel may reach another device: no remote copies, remote signals or barrier semaphores. Data moves between devices by JAX's collectives and lax.ppermute only.
A program may use at most 64 MiB of HBM per device.

```python
import jax
import jax.numpy as jnp
from jax import lax

D = 4096
DH = 256
TOK_DEV = 256
HEADS = 16
TOKENS = 8192


def shard_levels(own_key, dims, shards, low, top_value):
    loudness, own = 1.0, jax.random.fold_in(own_key, 6)
    for position, shards_of in shards:
        steps = jnp.exp(jax.random.uniform(jax.random.fold_in(own, position), (shards_of,), jnp.float32, low / len(shards), top_value / len(shards)))
        loudness = loudness * jnp.repeat(steps, dims[position] // shards_of).reshape([-1 if axis == position else 1 for axis in range(len(dims))])
    return loudness


def bell_draw(own_key, extent, width, most, shards=(), dtype=jnp.bfloat16):
    array = jax.random.normal(own_key, extent, jnp.float32) * width
    if len(shards) > 0:
        array = shard_levels(own_key, extent, shards, -0.22, 0.18) * array
    return jnp.clip(array, min=-most, max=most).astype(dtype)


def setup_inputs(seed: int = 0) -> dict:
    key_list = jax.random.split(jax.random.key(seed), 7)
    fwd_tokens = bell_draw(key_list[0], (TOKENS, D), 1.0, 6.0, ((0, 32),))
    bwd_tokens = bell_draw(key_list[1], (TOKENS, D), 1.0, 6.0, ((0, 32),))
    qkv_weight = bell_draw(key_list[2], (D, HEADS * 3 * DH), D ** -0.5, 0.09375, ((0, 32), (1, 16)))
    head_gain = jnp.clip(1.0 + 0.18 * jax.random.normal(key_list[3], (HEADS * DH,), jnp.float32), 0.1, 1.9)
    out_cotangent = bell_draw(key_list[4], (TOKENS, HEADS * DH), 1.0, 6.0, ((0, 32), (1, 16)), jnp.float32)
    initial_state = bell_draw(key_list[5], (2, HEADS, DH, DH), (DH // 8), 192.0, ((1, 16),), jnp.float32)
    return {"fwd_tokens": fwd_tokens, "bwd_tokens": bwd_tokens, "qkv_weight": qkv_weight, "head_gain": head_gain, "out_cotangent": out_cotangent, "initial_state": initial_state}


highest = lax.Precision.HIGHEST
epsilon = 1e-06

def span_forward(queries, keys, values, causal, carried):
    states = jnp.einsum('cti,ctj->cij', keys, values, precision=highest)
    prefix = jnp.cumsum(states, 0) - states + carried
    scores = jnp.einsum('cti,csi->cts', queries, keys, precision=highest) * causal
    output = jnp.einsum('cti,cij->ctj', queries, prefix, precision=highest) + jnp.einsum('cts,csj->ctj', scores, values, precision=highest)
    return (output, prefix, scores)

def head_pass(fwd_tokens, bwd_tokens, weight_head, gain_head, grad_head, carried):
    spans = TOKENS // TOK_DEV
    causal = jnp.tril(jnp.ones((TOK_DEV, TOK_DEV), jnp.float32))
    proj_fwd = jnp.dot(fwd_tokens, weight_head, preferred_element_type=jnp.float32).reshape(spans, TOK_DEV, 3 * DH)
    proj_bwd = jnp.dot(bwd_tokens, weight_head, preferred_element_type=jnp.float32).reshape(spans, TOK_DEV, 3 * DH)
    out_fwd, prefix_unused, scores_unused = span_forward(proj_fwd[..., :DH], proj_fwd[..., DH:2 * DH], proj_fwd[..., 2 * DH:], causal, carried[0])
    scale_fwd = lax.rsqrt(lax.optimization_barrier(jnp.mean(out_fwd * out_fwd, -1, keepdims=True)) + epsilon)
    normed = (out_fwd * scale_fwd * gain_head).reshape(TOKENS, DH)
    queries = proj_bwd[..., :DH]
    keys = proj_bwd[..., DH:2 * DH]
    values = proj_bwd[..., 2 * DH:]
    output, prefix, scores = span_forward(queries, keys, values, causal, carried[1])
    scale = lax.rsqrt(lax.optimization_barrier(jnp.mean(output * output, -1, keepdims=True)) + epsilon)
    weighted = grad_head.reshape(spans, TOK_DEV, DH) * gain_head
    d_out = scale * weighted - output * scale ** 3 * lax.optimization_barrier(jnp.mean(output * weighted, -1, keepdims=True))
    d_states = jnp.einsum('cti,ctj->cij', queries, d_out, precision=highest)
    suffix = jnp.cumsum(d_states[::-1], 0)[::-1] - d_states
    d_scores = jnp.einsum('ctj,csj->cts', d_out, values, precision=highest) * causal
    d_query = jnp.einsum('ctj,cij->cti', d_out, prefix, precision=highest) + jnp.einsum('cts,csi->cti', d_scores, keys, precision=highest)
    d_key = jnp.einsum('csj,cij->csi', values, suffix, precision=highest) + jnp.einsum('cts,cti->csi', d_scores, queries, precision=highest)
    d_value = jnp.einsum('csi,cij->csj', keys, suffix, precision=highest) + jnp.einsum('cts,ctj->csj', scores, d_out, precision=highest)
    d_proj = jnp.concatenate([d_query, d_key, d_value], -1).reshape(TOKENS, 3 * DH).astype(jnp.bfloat16)
    partial_value = jnp.dot(d_proj, weight_head.T, preferred_element_type=jnp.float32).astype(jnp.bfloat16)
    return (normed, partial_value)

def reference(fwd_tokens, bwd_tokens, qkv_weight, head_gain, out_cotangent, initial_state):
    weights = qkv_weight.reshape(D, HEADS, 3 * DH).transpose(1, 0, 2)
    gains = head_gain.reshape(HEADS, DH)
    grads = out_cotangent.reshape(TOKENS, HEADS, DH).transpose(1, 0, 2)
    carried = initial_state.transpose(1, 0, 2, 3)

    def step(total, items):
        normed, partial_value = head_pass(fwd_tokens, bwd_tokens, items[0], items[1], items[2], items[3])
        partial_value = lax.optimization_barrier(partial_value)
        return (total + partial_value.astype(jnp.float32), normed)
    total, normed = lax.scan(step, jnp.zeros((TOKENS, D), jnp.float32), (weights, gains, grads, carried))
    fwd_output = normed.transpose(1, 0, 2).reshape(TOKENS, HEADS * DH)
    return (fwd_output, total.astype(jnp.bfloat16))
```

```python
import functools

import jax
import jax.numpy as jnp
from jax import lax
from jax.experimental import pallas as pl
from jax.experimental.pallas import tpu as pltpu
from jax.sharding import Mesh
from jax.sharding import PartitionSpec as P


SEQ = ("y", "zh")
HEADS = ("zl", "x", "c")
DH = 256
EPS = 1e-06
BF = jnp.bfloat16
F32 = jnp.float32

NN = (((1,), (0,)), ((), ()))
NT = (((1,), (1,)), ((), ()))
TN = (((0,), (0,)), ((), ()))


def mm(a, b, dims):
    return lax.dot_general(a.astype(BF), b.astype(BF), dims, preferred_element_type=F32)


def ring(size, shift):
    return [(i, (i + shift) % size) for i in range(size)]


def shifted(value, axis, size, shift):
    return lax.ppermute(value, axis, ring(size, shift))


def causal(n):
    rows = lax.broadcasted_iota(jnp.int32, (n, n), 0)
    cols = lax.broadcasted_iota(jnp.int32, (n, n), 1)
    return cols <= rows


def states_kernel(proj_ref, out_ref):
    n = DH
    for m in range(2):
        keys = proj_ref[m * n : (m + 1) * n, n : 2 * n]
        values = proj_ref[m * n : (m + 1) * n, 2 * n :]
        out_ref[:, m * 8 : (m + 1) * 8, :] = mm(keys, values, TN).astype(BF).reshape(32, 8, n)


def scan_kernel(in_ref, out_ref, *, reverse):
    blocks = in_ref.shape[0]
    total = jnp.zeros(in_ref.shape[1:], F32)
    order = range(blocks - 1, -1, -1) if reverse else range(blocks)
    for b in order:
        out_ref[b] = total.astype(BF)
        total = total + in_ref[b].astype(F32)


def middle_kernel(
    proj_ref, prefix_ref, init_ref, cot_ref, gain_ref, fwd_ref, ds_ref, dq_ref, dk_ref, dv_ref
):
    n = DH
    mask = causal(n)
    gain = gain_ref[...]

    def block(m):
        queries = proj_ref[m * n : (m + 1) * n, :n].astype(BF)
        keys = proj_ref[m * n : (m + 1) * n, n : 2 * n].astype(BF)
        values = proj_ref[m * n : (m + 1) * n, 2 * n :].astype(BF)
        before = prefix_ref[:, m * 8 : (m + 1) * 8, :].astype(F32).reshape(n, n)
        prefix = (before + init_ref[m]).astype(BF)
        scores = jnp.where(mask, mm(queries, keys, NT), 0.0).astype(BF)
        output = mm(queries, prefix, NN) + mm(scores, values, NN)
        scale = lax.rsqrt(jnp.mean(output * output, -1, keepdims=True) + EPS)
        return queries, keys, values, prefix, scores, output, scale

    queries, keys, values, prefix, scores, output, scale = block(1)
    weighted = cot_ref[...] * gain
    d_out = scale * weighted - output * (
        scale * scale * scale * jnp.mean(output * weighted, -1, keepdims=True)
    )
    d_out = d_out.astype(BF)
    ds_ref[...] = mm(queries, d_out, TN).astype(BF).reshape(32, 8, n)
    d_scores = jnp.where(mask, mm(d_out, values, NT), 0.0).astype(BF)
    dq_ref[...] = (mm(d_out, prefix, NT) + mm(d_scores, keys, NN)).astype(BF)
    dk_ref[...] = mm(d_scores, queries, TN)
    dv_ref[...] = mm(scores, d_out, TN)
    _, _, _, _, _, output, scale = block(0)
    fwd_ref[...] = output * scale * gain


def last_kernel(proj_ref, suffix_ref, dq_ref, dk_ref, dv_ref, out_ref):
    n = DH
    keys = proj_ref[n : 2 * n, n : 2 * n].astype(BF)
    values = proj_ref[n : 2 * n, 2 * n :].astype(BF)
    suffix = suffix_ref[...].reshape(n, n)
    out_ref[:, :n] = dq_ref[...]
    out_ref[:, n : 2 * n] = (mm(values, suffix, NT) + dk_ref[...]).astype(BF)
    out_ref[:, 2 * n :] = (mm(keys, suffix, NN) + dv_ref[...]).astype(BF)


def scanned(slices, reverse):
    sent = lax.all_to_all(slices, SEQ, 0, 0, tiled=True)
    summed = pl.pallas_call(
        functools.partial(scan_kernel, reverse=reverse),
        out_shape=jax.ShapeDtypeStruct(sent.shape, BF),
    )(sent)
    return lax.all_to_all(summed, SEQ, 0, 0, tiled=True)


def weights_and_projection(tokens, weight):
    y, zh = lax.axis_index("y"), lax.axis_index("zh")
    rows, cols = weight.shape
    pieces = [(weight, 0)] + [(shifted(weight, "zh", 4, s), s) for s in (1, 3, 2)]
    block = jnp.zeros((4 * rows, cols), BF)
    for piece, s in pieces:
        block = lax.dynamic_update_slice(block, piece, ((zh - s) % 4 * rows, 0))
    span = 4 * rows
    half = span // 2
    total = jnp.zeros((tokens.shape[0], cols), F32)
    whole = jnp.zeros((8 * span, cols), BF)

    def add(total, whole, piece, start):
        part = lax.dynamic_slice(tokens, (0, start), (tokens.shape[0], piece.shape[0]))
        total = total + jnp.dot(part, piece, preferred_element_type=F32)
        return total, lax.dynamic_update_slice(whole, piece, (start, 0))

    total, whole = add(total, whole, block, y * span)
    up = down = block
    for k in range(1, 4):
        up, down = shifted(up, "y", 8, 1), shifted(down, "y", 8, -1)
        total, whole = add(total, whole, up, (y - k) % 8 * span)
        total, whole = add(total, whole, down, (y + k) % 8 * span)
    far_up = shifted(up[:half], "y", 8, 1)
    far_down = shifted(down[half:], "y", 8, -1)
    total, whole = add(total, whole, far_up, (y + 4) % 8 * span)
    total, whole = add(total, whole, far_down, (y + 4) % 8 * span + half)
    return total, whole


def body(fwd_tokens, bwd_tokens, qkv_weight, head_gain, out_cotangent, initial_state):
    n = DH
    tokens = jnp.concatenate([fwd_tokens, bwd_tokens], 0)
    proj, whole = weights_and_projection(tokens, qkv_weight)
    states = pl.pallas_call(
        states_kernel, out_shape=jax.ShapeDtypeStruct((32, 16, n), BF)
    )(proj)
    prefix = scanned(states, False)
    square = jax.ShapeDtypeStruct((n, n), F32)
    fwd_output, d_state, d_query, d_key, d_value = pl.pallas_call(
        middle_kernel,
        out_shape=(
            square,
            jax.ShapeDtypeStruct((32, 8, n), BF),
            jax.ShapeDtypeStruct((n, n), BF),
            square,
            square,
        ),
    )(proj, prefix, initial_state[:, 0], out_cotangent, head_gain[None, :])
    suffix = scanned(d_state, True)
    d_proj = pl.pallas_call(
        last_kernel, out_shape=jax.ShapeDtypeStruct((n, 3 * n), BF)
    )(proj, suffix, d_query, d_key, d_value)
    partial = lax.dot_general(whole, d_proj, NT, preferred_element_type=F32).astype(BF)
    partial = partial.reshape(8, 2, n, n)
    core = lax.axis_index("c")
    other = lax.dynamic_index_in_dim(partial, 1 - core, 1, keepdims=False)
    own = lax.dynamic_index_in_dim(partial, core, 1, keepdims=False)
    pair = own.astype(F32) + lax.ppermute(other, "c", [(0, 1), (1, 0)]).astype(F32)
    tiles = lax.all_to_all(pair.astype(BF), ("zl", "x"), 0, 0, tiled=True)
    grad_t = jnp.sum(tiles.astype(F32), axis=0)
    return fwd_output, grad_t.T.astype(BF)


def solution(mesh):
    finer = Mesh(mesh.devices.reshape(8, 4, 2, 4, 2), ("y", "zh", "zl", "x", "c"))
    return jax.shard_map(
        body,
        mesh=finer,
        in_specs=(
            P(SEQ, None),
            P(SEQ, None),
            P(SEQ, HEADS),
            P(HEADS),
            P(SEQ, HEADS),
            P(None, HEADS, None, None),
        ),
        out_specs=(P(SEQ, HEADS), P(SEQ, HEADS)),
        check_vma=False,
    )
```

```python
import functools

import jax
import jax.numpy as jnp
from jax import lax
from jax.experimental import pallas as pl
from jax.experimental.pallas import tpu as pltpu
from jax.sharding import Mesh
from jax.sharding import PartitionSpec as P


SEQ = ("y", "zh")
HEADS = ("zl", "x", "c")
DH = 256
EPS = 1e-06
BF = jnp.bfloat16
F32 = jnp.float32

SMALL = pltpu.CompilerParams(vmem_limit_bytes=16 * 1024 * 1024)
NN = (((1,), (0,)), ((), ()))
NT = (((1,), (1,)), ((), ()))
TN = (((0,), (0,)), ((), ()))


def mm(a, b, dims):
    return lax.dot_general(a.astype(BF), b.astype(BF), dims, preferred_element_type=F32)


def ring(size, shift):
    return [(i, (i + shift) % size) for i in range(size)]


def shifted(value, axis, size, shift):
    return lax.ppermute(value, axis, ring(size, shift))


def causal(n):
    rows = lax.broadcasted_iota(jnp.int32, (n, n), 0)
    cols = lax.broadcasted_iota(jnp.int32, (n, n), 1)
    return cols <= rows


def states_kernel(sum_ref, tokens_ref, up_ref, down_ref, kv_ref, out_ref):
    n = DH
    half = up_ref.shape[0]
    kv = sum_ref[...] + mm(tokens_ref[:, :half], up_ref[...], NN)
    kv = (kv + mm(tokens_ref[:, half:], down_ref[...], NN)).astype(BF)
    kv_ref[...] = kv
    for m in range(2):
        keys, values = kv[m * n : (m + 1) * n, :n], kv[m * n : (m + 1) * n, n:]
        out_ref[:, m * 8 : (m + 1) * 8, :] = mm(keys, values, TN).astype(BF).reshape(32, 8, n)


def scan_kernel(in_ref, out_ref, *, reverse):
    blocks = in_ref.shape[0]
    total = jnp.zeros(in_ref.shape[1:], F32)
    order = range(blocks - 1, -1, -1) if reverse else range(blocks)
    for b in order:
        out_ref[b] = total.astype(BF)
        total = total + in_ref[b].astype(F32)


def middle_kernel(
    queries_ref, kv_ref, prefix_ref, init_ref, cot_ref, gain_ref, fwd_ref, ds_ref, dq_ref, dk_ref, dv_ref
):
    n = DH
    mask = causal(n)
    gain = gain_ref[...]

    def block(m):
        queries = queries_ref[m * n : (m + 1) * n, :]
        keys, values = kv_ref[m * n : (m + 1) * n, :n], kv_ref[m * n : (m + 1) * n, n:]
        before = prefix_ref[:, m * 8 : (m + 1) * 8, :].astype(F32).reshape(n, n)
        prefix = (before + init_ref[m]).astype(BF)
        scores = jnp.where(mask, mm(queries, keys, NT), 0.0).astype(BF)
        output = mm(queries, prefix, NN) + mm(scores, values, NN)
        scale = lax.rsqrt(jnp.mean(output * output, -1, keepdims=True) + EPS)
        return queries, keys, values, prefix, scores, output, scale

    queries, keys, values, prefix, scores, output, scale = block(1)
    weighted = cot_ref[...] * gain
    d_out = scale * weighted - output * (
        scale * scale * scale * jnp.mean(output * weighted, -1, keepdims=True)
    )
    d_out = d_out.astype(BF)
    ds_ref[...] = mm(queries, d_out, TN).astype(BF).reshape(32, 8, n)
    d_scores = jnp.where(mask, mm(d_out, values, NT), 0.0).astype(BF)
    dq_ref[...] = (mm(d_out, prefix, NT) + mm(d_scores, keys, NN)).astype(BF)
    dk_ref[...] = mm(d_scores, queries, TN)
    dv_ref[...] = mm(scores, d_out, TN)
    _, _, _, _, _, output, scale = block(0)
    fwd_ref[...] = output * scale * gain


def last_kernel(kv_ref, suffix_ref, dq_ref, dk_ref, dv_ref, out_ref):
    n = DH
    keys, values = kv_ref[n:, :n], kv_ref[n:, n:]
    suffix = suffix_ref[...].reshape(n, n)
    out_ref[:, :n] = dq_ref[...]
    out_ref[:, n : 2 * n] = (mm(values, suffix, NT) + dk_ref[...]).astype(BF)
    out_ref[:, 2 * n :] = (mm(keys, suffix, NN) + dv_ref[...]).astype(BF)


def scanned(slices, reverse):
    sent = lax.all_to_all(slices, SEQ, 0, 0, tiled=True)
    summed = pl.pallas_call(
        functools.partial(scan_kernel, reverse=reverse),
        out_shape=jax.ShapeDtypeStruct(sent.shape, BF),
        compiler_params=SMALL,
    )(sent)
    return lax.all_to_all(summed, SEQ, 0, 0, tiled=True)


def stored(whole, piece, core, y, col):
    halves = piece.reshape(2, DH, piece.shape[1])
    for k in range(2):
        part = lax.dynamic_index_in_dim(halves, core ^ k, 0, keepdims=False)
        whole = lax.dynamic_update_slice(whole, part[None, None], (k, y, 0, col))
    return whole


def body(fwd_tokens, bwd_tokens, qkv_weight, head_gain, out_cotangent, initial_state):
    n = DH
    y, zh, core = lax.axis_index("y"), lax.axis_index("zh"), lax.axis_index("c")
    rows = qkv_weight.shape[0]
    span = 4 * rows
    half = span // 2
    w_q, w_kv = qkv_weight[:, :n], qkv_weight[:, n:]

    pieces = [(w_kv, 0)] + [(shifted(w_kv, "zh", 4, s), s) for s in (2, 1, 3)]
    q_line = lax.all_to_all(jnp.broadcast_to(w_q[None], (8, rows, n)), "y", 0, 0, tiled=True)
    block = jnp.zeros((span, 2 * n), BF)
    for piece, s in pieces:
        block = lax.dynamic_update_slice(block, piece, ((zh - s) % 4 * rows, 0))
    q_lines = [(q_line, 0)] + [(shifted(q_line, "zh", 4, s), s) for s in (2, 1, 3)]

    tokens = jnp.concatenate([fwd_tokens, bwd_tokens], 0)
    whole = jnp.zeros((2, 8, n, 3 * n), BF)

    def columns(at):
        return lax.dynamic_slice(tokens, (0, at * span), (tokens.shape[0], span))

    def add(total, whole, piece, at):
        total = total + jnp.dot(columns(at), piece, preferred_element_type=F32)
        return total, stored(whole, piece, core, at, n)

    total, whole = add(jnp.zeros((2 * n, 2 * n), F32), whole, block, y)
    up = down = block
    for k in range(1, 4):
        up, down = shifted(up, "y", 8, 1), shifted(down, "y", 8, -1)
        total, whole = add(total, whole, up, (y - k) % 8)
        total, whole = add(total, whole, down, (y + k) % 8)
    far = (y + 4) % 8
    far_up = shifted(up[:half], "y", 8, 1)
    far_down = shifted(down[half:], "y", 8, -1)
    kv, states = pl.pallas_call(
        states_kernel,
        out_shape=(
            jax.ShapeDtypeStruct((2 * n, 2 * n), BF),
            jax.ShapeDtypeStruct((32, 16, n), BF),
        ),
        compiler_params=SMALL,
    )(total, columns(far), far_up, far_down)
    whole = stored(whole, jnp.concatenate([far_up, far_down], 0), core, far, n)
    prefix = scanned(states, False)

    w_queries = jnp.zeros((8, 4, rows, n), BF)
    held, whole, _ = lax.optimization_barrier(([p for p, _ in q_lines], whole, states))
    for piece, s in zip(held, [s for _, s in q_lines]):
        at = (zh - s) % 4
        w_queries = lax.dynamic_update_slice(w_queries, piece[:, None], (0, at, 0, 0))
        whole = lax.dynamic_update_slice(
            whole, piece[None], ((at // 2) ^ core, 0, (at % 2) * rows, 0)
        )
    queries = jnp.dot(tokens, w_queries.reshape(8 * span, n), preferred_element_type=F32)

    square = jax.ShapeDtypeStruct((n, n), F32)
    fwd_output, d_state, d_query, d_key, d_value = pl.pallas_call(
        middle_kernel,
        out_shape=(
            square,
            jax.ShapeDtypeStruct((32, 8, n), BF),
            jax.ShapeDtypeStruct((n, n), BF),
            square,
            square,
        ),
        compiler_params=SMALL,
    )(queries.astype(BF), kv, prefix, initial_state[:, 0], out_cotangent, head_gain[None, :])
    suffix = scanned(d_state, True)
    d_proj = pl.pallas_call(
        last_kernel,
        out_shape=jax.ShapeDtypeStruct((n, 3 * n), BF),
        compiler_params=SMALL,
    )(kv, suffix, d_query, d_key, d_value)

    def partial(side):
        flat = whole[side].reshape(8 * n, 3 * n)
        return lax.dot_general(flat, d_proj, NT, preferred_element_type=F32).astype(BF)

    swapped = lax.ppermute(partial(1), "c", [(0, 1), (1, 0)])
    own = lax.optimization_barrier(partial(0))
    pair = own.astype(F32) + swapped.astype(F32)
    tiles = lax.all_to_all(pair.astype(BF).reshape(8, n, n), ("zl", "x"), 0, 0, tiled=True)
    grad_t = jnp.sum(tiles.astype(F32), axis=0)
    return fwd_output, grad_t.T.astype(BF)


def solution(mesh):
    finer = Mesh(mesh.devices.reshape(8, 4, 2, 4, 2), ("y", "zh", "zl", "x", "c"))
    return jax.shard_map(
        body,
        mesh=finer,
        in_specs=(
            P(SEQ, None),
            P(SEQ, None),
            P(SEQ, HEADS),
            P(HEADS),
            P(SEQ, HEADS),
            P(None, HEADS, None, None),
        ),
        out_specs=(P(SEQ, HEADS), P(SEQ, HEADS)),
        check_vma=False,
    )
```
